1024 devices in a mesh: group: 128 (over x, y, core), tensor: 8 (over z).
Axes of the slice: x: 8, y: 8, z: 8, core: 2. Of those that a mesh axis runs over, the one named last changes fastest.
Arguments:
- queries: bfloat16 [49152, 4096], P('group', 'tensor')
- text_kv: bfloat16 [49152, 2048], P('group', 'tensor')
- out_grad: bfloat16 [49152, 4096], P('group', 'tensor'), may hold values from -6 to 6
- text_segment: int32 [128, 384], P('group'), may hold values from 0 to 7, never falling along the last dimension, each value on 1 to 96 neighbouring positions
- visual_rows: bfloat16 [16384, 8192], P('group', 'tensor'), may hold values from -6 to 6
- kv_weight: bfloat16 [8192, 2048], P('tensor'), may hold values from -0.0625 to 0.0625
- visual_dest: int32 [16384, 1], P('group'), may hold values from 0 to 127, as said below
- visual_sample: int32 [16384], P('group'), may hold values from 0 to 7, as said below
Outputs:
- attended: bfloat16 [49152, 4096], P('group', 'tensor')
- query_grad: bfloat16 [49152, 4096], P('group', 'tensor')
- text_kv_grad: bfloat16 [49152, 2048], P('group', 'tensor')
- visual_grad: bfloat16 [16384, 8192], P('group', 'tensor')
The draws below stay inside these ranges and needn't reach their ends.
Inputs may be any that keep to these rules, and one draw needn't show every extreme that they name: `visual_dest`: a group's rows come in aligned runs of 2 rows, each run to one pack, the runs of one group to distinct packs, so exactly 2 rows of a group reach each pack that it names and none reach the others. `visual_sample`: one sample for all rows of a run. `text_segment`: never falling along a pack, each sample at most 96 tokens.
All inputs are finite; a program needn't handle non-finite values.
Results may differ from the reference program's by a relative error of at most 0.015.
Values may be sent and summed in bfloat16 or wider, within the bound.
A program may use at most 64 MiB of HBM per device.

```python
import math
import jax
import jax.numpy as jnp
import numpy as np
from jax import lax

D = 8192
KVH = 8
HD = 128
QPK = 4
QH = 32
PACK = 384
VIS_DEV = 128
SEGS = 8
SEG_MOST = 96
CAP = 2
TEXT = 49152
VIS = 16384
N_GROUP = 128


def text_pair(key):
    base = jax.random.fold_in(key, 11)
    kv_full = jax.random.normal(jax.random.fold_in(base, 1), (TEXT, 2 * KVH * HD), jnp.float32)
    query_full = jax.random.normal(jax.random.fold_in(base, 2), (TEXT, QPK * KVH * HD), jnp.float32)
    return (query_full, kv_full)


def draw_queries(key, part):
    return text_pair(key)[0].astype(jnp.bfloat16)


def draw_text_kv(key, part):
    return text_pair(key)[1].astype(jnp.bfloat16)


def draw_visual_dest(key, part):
    base = jax.random.fold_in(key, 23)
    run_count = VIS_DEV // CAP
    group_keys = jax.random.split(jax.random.fold_in(base, 1), N_GROUP)
    orders = jax.vmap(lambda one: jax.random.permutation(one, N_GROUP))(group_keys)[:, :run_count]
    return jnp.repeat(orders.astype(jnp.int32), CAP, axis=1).reshape(VIS, 1)


def draw_visual_sample(key, part):
    base = jax.random.fold_in(key, 29)
    run_count = VIS_DEV // CAP
    samples = jax.random.randint(jax.random.fold_in(base, 1), (N_GROUP * run_count,), 0, SEGS, dtype=jnp.int32)
    return jnp.repeat(samples, CAP).astype(jnp.int32)


def level_of(rng, extent, cuts, low, largest):
    def one(axis_at, shards_of):
        draws = jax.random.uniform(jax.random.fold_in(jax.random.fold_in(rng, 6), axis_at), (shards_of,), jnp.float32, low / len(cuts), largest / len(cuts))
        return jnp.repeat(jnp.exp(draws), extent[axis_at] // shards_of).reshape((-1,) + (1,) * (len(extent) - axis_at - 1))

    gain = one(*cuts[0])
    for cut in cuts[1:]:
        gain = gain * one(*cut)
    return gain


def split_up(number_of, total, reach, skew):
    portions = [(1 << 20) // math.isqrt(grade ** skew) + 1 for grade in range(2, number_of + 1)]
    surplus, given = total - reach - (number_of - 1), [1] * (number_of - 1)
    while surplus > 0:
        free = [i for i in range(number_of - 1) if given[i] < reach]
        pool, budget = sum([portions[i] for i in free]), surplus
        for i in free:
            more = min(reach - given[i], max(1, budget * portions[i] // pool), surplus)
            given[i] = given[i] + more
            surplus = surplus - more
    return np.array([reach] + given)


def uneven(rng, number_of, total, limit, slope):
    if number_of == 2:
        one = jax.random.randint(rng, (), max(1, total - limit), min(limit, total - 1) + 1)
        return jnp.stack([one, total - one])
    tallies = jnp.asarray(split_up(number_of, total, limit, slope), jnp.int32)
    pairs = (number_of - 1) // 2
    donor, taker = tallies[1:1 + 2 * pairs:2], tallies[2:2 + 2 * pairs:2]
    room = jnp.minimum(donor - 1, limit - taker)
    moved = jax.random.randint(jax.random.fold_in(rng, 1), (pairs,), 0, 1 << 20) % (room + 1)
    tallies = tallies.at[1:1 + 2 * pairs:2].set(donor - moved).at[2:2 + 2 * pairs:2].set(taker + moved)
    return tallies[jax.random.permutation(jax.random.fold_in(rng, 2), number_of)]


def bell_draw(rng, dims, deviation, bound, cuts=(), kind=jnp.bfloat16):
    factor_of = level_of(rng, dims, cuts, -0.22, 0.18) if cuts else 1.0
    entries = jax.random.normal(rng, dims, jnp.float32) * deviation * factor_of
    return jnp.minimum(jnp.maximum(entries, -bound), bound).astype(kind)


def setup_inputs(seed: int = 0) -> dict:
    arg_keys = jax.random.split(jax.random.key(seed), 9)
    queries = draw_queries(jax.random.fold_in(arg_keys[8], 71), 0)
    text_kv = draw_text_kv(jax.random.fold_in(arg_keys[8], 71), 0)
    out_grad = bell_draw(arg_keys[2], (TEXT, QH * HD), 1.0, 6.0, ((0, 128), (1, 8)))
    text_segment = jax.vmap(lambda own: jnp.searchsorted(jnp.cumsum(uneven(own, SEGS, PACK, SEG_MOST, 1)), jnp.arange(PACK), side="right"))(jax.random.split(arg_keys[3], N_GROUP)).reshape((N_GROUP, PACK)).astype(jnp.int32)
    visual_rows = bell_draw(arg_keys[4], (VIS, D), 1.0, 6.0, ((0, 128), (1, 8)))
    kv_weight = bell_draw(arg_keys[5], (D, 2 * KVH * HD), D ** -0.5, 0.0625, ((0, 8),))
    visual_dest = draw_visual_dest(jax.random.fold_in(arg_keys[8], 71), 0)
    visual_sample = draw_visual_sample(jax.random.fold_in(arg_keys[8], 71), 0)
    return {"queries": queries, "text_kv": text_kv, "out_grad": out_grad, "text_segment": text_segment, "visual_rows": visual_rows, "kv_weight": kv_weight, "visual_dest": visual_dest, "visual_sample": visual_sample}


def to_bf16_and_back(values):
    return lax.optimization_barrier(values.astype(jnp.bfloat16)).astype(jnp.float32)

def slot_index(visual_dest):
    destination = visual_dest[:, 0].reshape(N_GROUP, VIS_DEV)
    onehot = (destination[:, :, None] == jnp.arange(N_GROUP, dtype=jnp.int32)[None, None, :]).astype(jnp.int32)
    earlier = jnp.cumsum(onehot, axis=1) - onehot
    rank = lax.optimization_barrier(jnp.sum(earlier * onehot, axis=2))
    source = jnp.arange(N_GROUP, dtype=jnp.int32)[:, None]
    slot = source * CAP + rank
    return (destination.reshape(-1).astype(jnp.int32), slot.reshape(-1).astype(jnp.int32))

def attend_pack(pack):
    queries, text_kv, out_grad, segment, vis_kv, vis_sample = pack
    length = queries.shape[0]
    scale = 1.0 / math.sqrt(HD)
    query_heads = queries.astype(jnp.float32).reshape(length, KVH, QPK, HD)
    grad_heads = out_grad.astype(jnp.float32).reshape(length, KVH, QPK, HD)
    text_heads = text_kv.reshape(length, KVH, 2, HD)
    vis_heads = vis_kv.reshape(vis_kv.shape[0], KVH, 2, HD)
    keys = jnp.concatenate([text_heads[:, :, 0], vis_heads[:, :, 0]], axis=0).astype(jnp.float32)
    values = jnp.concatenate([text_heads[:, :, 1], vis_heads[:, :, 1]], axis=0).astype(jnp.float32)
    places = jnp.arange(length, dtype=jnp.int32)
    text_mask = (segment[:, None] == segment[None, :]) & (places[None, :] <= places[:, None])
    vis_mask = vis_sample[None, :] == segment[:, None]
    mask = jnp.concatenate([text_mask, vis_mask], axis=1)
    scores = jnp.einsum('pgjd,kgd->gjpk', query_heads, keys) * scale
    top = lax.optimization_barrier(jnp.max(jnp.where(mask, scores, -jnp.inf), axis=-1, keepdims=True))
    expo = jnp.where(mask, jnp.exp(scores - top), 0.0)
    probs = expo / lax.optimization_barrier(jnp.sum(expo, axis=-1, keepdims=True))
    weights = to_bf16_and_back(probs)
    attended = jnp.einsum('gjpk,kgd->pgjd', weights, values).astype(jnp.bfloat16)
    dprobs = jnp.einsum('pgjd,kgd->gjpk', grad_heads, values)
    inner = lax.optimization_barrier(jnp.sum(probs * dprobs, axis=-1, keepdims=True))
    dscores = to_bf16_and_back(probs * (dprobs - inner) * scale)
    query_grad = jnp.einsum('gjpk,kgd->pgjd', dscores, keys).astype(jnp.bfloat16)
    key_grad = jnp.einsum('gjpk,pgjd->kgd', dscores, query_heads).astype(jnp.bfloat16)
    value_grad = jnp.einsum('gjpk,pgjd->kgd', weights, grad_heads).astype(jnp.bfloat16)
    kv_grad = jnp.stack([key_grad, value_grad], axis=2)
    text_grad = kv_grad[:length].reshape(length, -1)
    vis_grad = kv_grad[length:].reshape(vis_kv.shape[0], -1)
    return (attended.reshape(length, -1), query_grad.reshape(length, -1), text_grad, vis_grad)

def reference(queries, text_kv, out_grad, text_segment, visual_rows, kv_weight, visual_dest, visual_sample):
    visual_kv = jnp.dot(visual_rows, kv_weight, preferred_element_type=jnp.float32).astype(jnp.bfloat16)
    destination, slot = slot_index(visual_dest)
    width = visual_kv.shape[1]
    buffer = jnp.zeros((N_GROUP, N_GROUP * CAP, width), jnp.bfloat16).at[destination, slot].set(visual_kv)
    tags = jnp.full((N_GROUP, N_GROUP * CAP), -1, jnp.int32).at[destination, slot].set(visual_sample)
    packs = (queries.reshape(N_GROUP, PACK, -1), text_kv.reshape(N_GROUP, PACK, -1), out_grad.reshape(N_GROUP, PACK, -1), text_segment, buffer, tags)
    attended, query_grad, text_grad, vis_grad = lax.map(attend_pack, packs)
    visual_kv_grad = vis_grad[destination, slot]
    visual_grad = jnp.dot(visual_kv_grad, kv_weight.T, preferred_element_type=jnp.float32).astype(jnp.bfloat16)
    return (attended.reshape(TEXT, -1), query_grad.reshape(TEXT, -1), text_grad.reshape(TEXT, -1), visual_grad)
```

```python
import functools
import math

import jax
import jax.numpy as jnp
from jax import lax
from jax.experimental import pallas as pl
from jax.experimental.pallas import tpu as pltpu
from jax.sharding import PartitionSpec as P

MESH = pl.DeviceIdType.MESH
HD = 128
QPK = 4
PACK = 384
BLK = 128
NZ = 8
NG = 128
ROWS = 128
SLOTS = 256
CHUNKS = 2
OFFSETS = (-4, 3, -3, 2, -2, 1, -1, 0)
SCALE = 1.0 / math.sqrt(HD)
F32 = jnp.float32
BF16 = jnp.bfloat16


def dot_nn(a, b):
    return lax.dot_general(a, b, (((1,), (0,)), ((), ())), preferred_element_type=F32)


def dot_nt(a, b):
    return lax.dot_general(a, b, (((1,), (1,)), ((), ())), preferred_element_type=F32)


def dot_tn(a, b):
    return lax.dot_general(a, b, (((0,), (0,)), ((), ())), preferred_element_type=F32)


def iota(shape, dim):
    return lax.broadcasted_iota(jnp.int32, shape, dim)


def column_of(row):
    n = row.shape[1]
    eye = iota((n, n), 0) == iota((n, n), 1)
    return jnp.sum(jnp.where(eye, row, 0.0), axis=1, keepdims=True)


def key_range(block):
    low = max(0, (block - 1) * BLK)
    return low, (block + 1) * BLK - low


def kernel(
    q_hbm, kv_hbm, og_hbm, seg_ref, rows_hbm, w_hbm, dest_ref, sample_ref,
    att_ref, qg_ref, tg_ref, vg_ref,
    w_v, rows_v, q_v, kv_v, og_v,
    part, send_a, recv_a, send_b, recv_b,
    tag_s, tag_r, fwd_s, fwd_r, bwd_s, bwd_r,
    own_kvg, ag_a, ag_b, acc,
    tmask, vmask, exp_t, dp_t, stats, p_vis, ds_vis, kv_vis, dkv_vis, dk_t, dv_t,
    w_sem, in_sem, sa_sem, ra_sem, sb_sem, rb_sem,
    a2a_sem, self_sem, ga_s, ga_r, gb_s, gb_r,
):
    g = lax.axis_index("group")
    t = lax.axis_index("tensor")
    gx, gy, gc = g // 16, (g // 2) % 8, g % 2
    left, right = (t + NZ - 1) % NZ, (t + 1) % NZ

    def peer(k):
        pair, other = k // 2, k % 2
        kx, ky = pair % 8, pair // 8
        dx = 4 + (2 * (kx % 2) - 1) * ((kx + 1) // 2)
        dy = 4 + (2 * (ky % 2) - 1) * ((ky + 1) // 2)
        return ((gx + dx + 8) % 8) * 16 + ((gy + dy + 8) % 8) * 2 + (gc + 1 + other) % 2

    barrier = pltpu.get_barrier_semaphore()

    def greet(k, carry):
        pl.semaphore_signal(barrier, inc=1, device_id={"group": peer(k)}, device_id_type=MESH)
        return carry

    lax.fori_loop(0, NG - 1, greet, 0)
    for near in (left, right):
        pl.semaphore_signal(barrier, inc=1, device_id={"tensor": near}, device_id_type=MESH)

    rows_in = pltpu.make_async_copy(rows_hbm, rows_v, in_sem.at[0])
    rows_in.start()
    w_in = []
    for i, off in enumerate(OFFSETS):
        column = pl.multiple_of(((t + off + NZ) % NZ) * 2 * HD, 2 * HD)
        copy = pltpu.make_async_copy(w_hbm.at[:, pl.ds(column, 2 * HD)], w_v.at[i], w_sem.at[i])
        copy.start()
        w_in.append(copy)
    other_in = [
        pltpu.make_async_copy(kv_hbm, kv_v, in_sem.at[1]),
        pltpu.make_async_copy(q_hbm, q_v, in_sem.at[2]),
        pltpu.make_async_copy(og_hbm, og_v, in_sem.at[3]),
    ]
    for copy in other_in:
        copy.start()

    dest_row = dest_ref[...].astype(F32)
    dest_col = column_of(dest_row)
    sample_col = column_of(sample_ref[...].astype(F32))
    pack_row = iota((ROWS, NG), 1).astype(F32)
    tag_s[0] = jnp.max(
        jnp.where(dest_col == pack_row, sample_col, -1.0), axis=0, keepdims=True
    )
    parity_row = (iota((1, ROWS), 1) % 2).astype(F32)
    place_out = (iota((SLOTS, ROWS), 0).astype(F32) == dest_row * 2.0 + parity_row).astype(BF16)
    parity_col = (iota((ROWS, 1), 0) % 2).astype(F32)
    place_back = (iota((ROWS, SLOTS), 1).astype(F32) == dest_col * 2.0 + parity_col).astype(BF16)

    seg_row = seg_ref[...].astype(F32)
    for block in range(PACK // BLK):
        low, n = key_range(block)
        seg_key = column_of(seg_row[:, low : low + n])
        seg_tok = seg_row[:, block * BLK : (block + 1) * BLK]
        before = iota((n, BLK), 0) + low <= iota((n, BLK), 1) + block * BLK
        tmask[block, 0:n, :] = jnp.where((seg_key == seg_tok) & before, 1.0, 0.0)

    rows_in.wait()
    for i in range(len(OFFSETS)):
        w_in[i].wait()
        part[i] = dot_nn(rows_v[...], w_v[i])

    pl.semaphore_wait(barrier, NG + 1)

    size = ROWS // CHUNKS

    def hop(src, dst, ssem, rsem, near):
        return pltpu.make_async_remote_copy(
            src_ref=src, dst_ref=dst, send_sem=ssem, recv_sem=rsem,
            device_id={"tensor": near}, device_id_type=MESH,
        )

    def rs_copy(side, step, c):
        at = pl.ds(c * size, size)
        if side == 0:
            return hop(send_a.at[step, at], recv_a.at[step, at], sa_sem.at[step, c], ra_sem.at[step, c], left)
        return hop(send_b.at[step, at], recv_b.at[step, at], sb_sem.at[step, c], rb_sem.at[step, c], right)

    sides = ((0, 4, send_a, recv_a), (1, 3, send_b, recv_b))
    started = []

    def rs_step(step):
        for c in range(CHUNKS):
            lo, hi = c * size, (c + 1) * size
            for side, steps, send, recv in sides:
                if step >= steps:
                    continue
                off = step - 4 if side == 0 else 3 - step
                value = part[OFFSETS.index(off), lo:hi, :]
                if step > 0:
                    rs_copy(side, step - 1, c).wait_recv()
                    value = value + recv[step - 1, lo:hi, :].astype(F32)
                send[step, lo:hi, :] = value.astype(BF16)
                copy = rs_copy(side, step, c)
                copy.start()
                started.append(copy)

    def send_all(source, landing, ssem, rsem):
        def body(k, carry):
            p = peer(k)
            pltpu.make_async_remote_copy(
                src_ref=source(p), dst_ref=landing.at[g], send_sem=ssem, recv_sem=rsem,
                device_id={"group": p}, device_id_type=MESH,
            ).start()
            return carry

        lax.fori_loop(0, NG - 1, body, 0)

    def wait_all(buffer, sem):
        view = buffer.at[pl.ds(0, NG - 1)]
        pltpu.make_async_copy(view, view, sem).wait()

    def text_head(h):
        for block in range(PACK // BLK):
            low, n = key_range(block)
            tok = slice(block * BLK, (block + 1) * BLK)
            lanes = slice(h * HD, (h + 1) * HD)
            scores = dot_nt(kv_v[low : low + n, 0:HD], q_v[tok, lanes]) * SCALE
            scores = jnp.where(tmask[block, 0:n, :] > 0.5, scores, -jnp.inf)
            top = jnp.max(scores, axis=0, keepdims=True)
            expo = jnp.exp(scores - top)
            dprobs = dot_nt(kv_v[low : low + n, HD : 2 * HD], og_v[tok, lanes])
            exp_t[h, block, 0:n, :] = expo
            dp_t[h, block, 0:n, :] = dprobs
            stats[h, 0:1, tok] = top
            stats[h, 1:2, tok] = jnp.sum(expo, axis=0, keepdims=True)
            stats[h, 2:3, tok] = jnp.sum(expo * dprobs, axis=0, keepdims=True)

    rs_step(0)
    send_all(lambda p: tag_s.at[0], tag_r, a2a_sem.at[0], a2a_sem.at[1])
    tag_r[g] = tag_s[0]
    for copy in other_in:
        copy.wait()
    text_head(0)
    rs_step(1)
    text_head(1)
    rs_step(2)
    text_head(2)
    rs_step(3)
    text_head(3)

    wait_all(tag_s_view(tag_r), a2a_sem.at[0])
    wait_all(tag_r, a2a_sem.at[1])
    table = tag_r[...].reshape(NG, NG).astype(BF16)
    spread = (iota((SLOTS, NG), 0) // 2 == iota((SLOTS, NG), 1)).astype(BF16)
    by_slot = dot_nn(spread, table).astype(BF16)
    mine = (iota((NG, PACK), 0) == g).astype(BF16)
    vmask[...] = jnp.where(dot_nn(by_slot, mine) == seg_row, 1.0, 0.0)

    for c in range(CHUNKS):
        rs_copy(0, 3, c).wait_recv()
        rs_copy(1, 2, c).wait_recv()
    own = (part[OFFSETS.index(0)] + recv_a[3].astype(F32)) + recv_b[2].astype(F32)
    fwd_s[...] = dot_nn(place_out, own.astype(BF16)).reshape(NG, 2, 2 * HD).astype(BF16)
    to_self = pltpu.make_async_copy(fwd_s.at[g], fwd_r.at[g], self_sem.at[0])
    to_self.start()
    send_all(lambda p: fwd_s.at[p], fwd_r, a2a_sem.at[2], a2a_sem.at[3])
    to_self.wait()
    wait_all(fwd_s, a2a_sem.at[2])
    wait_all(fwd_r, a2a_sem.at[3])

    kv_vis[...] = fwd_r[...].astype(F32).reshape(SLOTS, 2 * HD).astype(BF16)
    for h in range(QPK):
        lanes = slice(h * HD, (h + 1) * HD)
        q_h, og_h = q_v[:, lanes], og_v[:, lanes]
        scores = dot_nt(kv_vis[:, 0:HD], q_h) * SCALE
        scores = jnp.where(vmask[...] > 0.5, scores, -jnp.inf)
        top_t = stats[h, 0:1, :]
        top = jnp.maximum(jnp.max(scores, axis=0, keepdims=True), top_t)
        expo = jnp.exp(scores - top)
        again = jnp.exp(top_t - top)
        dprobs = dot_nt(kv_vis[:, HD : 2 * HD], og_h)
        total = stats[h, 1:2, :] * again + jnp.sum(expo, axis=0, keepdims=True)
        over = 1.0 / total
        inner = (stats[h, 2:3, :] * again + jnp.sum(expo * dprobs, axis=0, keepdims=True)) * over
        probs = expo * over
        weights = probs.astype(BF16)
        dscores = (probs * (dprobs - inner) * SCALE).astype(BF16)
        p_vis[h] = weights
        ds_vis[h] = dscores
        stats[h, 3:4, :] = again * over
        stats[h, 4:5, :] = inner
        dk = dot_nn(dscores, q_h)
        dv = dot_nn(weights, og_h)
        if h == 0:
            dkv_vis[:, 0:HD] = dk
            dkv_vis[:, HD : 2 * HD] = dv
        else:
            dkv_vis[:, 0:HD] += dk
            dkv_vis[:, HD : 2 * HD] += dv

    bwd_s[...] = dkv_vis[...].reshape(NG, 2, 2 * HD).astype(BF16)
    to_self = pltpu.make_async_copy(bwd_s.at[g], bwd_r.at[g], self_sem.at[1])
    to_self.start()
    send_all(lambda p: bwd_s.at[p], bwd_r, a2a_sem.at[4], a2a_sem.at[5])

    dk_t[...] = jnp.zeros_like(dk_t)
    dv_t[...] = jnp.zeros_like(dv_t)
    for h in range(QPK):
        for block in range(PACK // BLK):
            low, n = key_range(block)
            tok = slice(block * BLK, (block + 1) * BLK)
            lanes = slice(h * HD, (h + 1) * HD)
            probs = exp_t[h, block, 0:n, :] * stats[h, 3:4, tok]
            weights = probs.astype(BF16)
            dscores = (probs * (dp_t[h, block, 0:n, :] - stats[h, 4:5, tok]) * SCALE).astype(BF16)
            dk_t[low : low + n, :] += dot_nn(dscores, q_v[tok, lanes])
            dv_t[low : low + n, :] += dot_nn(weights, og_v[tok, lanes])
            out = dot_tn(weights, kv_v[low : low + n, HD : 2 * HD])
            out = out + dot_tn(p_vis[h, :, tok], kv_vis[:, HD : 2 * HD])
            att_ref[tok, lanes] = out.astype(BF16)
            dq = dot_tn(dscores, kv_v[low : low + n, 0:HD])
            dq = dq + dot_tn(ds_vis[h, :, tok], kv_vis[:, 0:HD])
            qg_ref[tok, lanes] = dq.astype(BF16)
    tg_ref[:, 0:HD] = dk_t[...].astype(BF16)
    tg_ref[:, HD : 2 * HD] = dv_t[...].astype(BF16)

    to_self.wait()
    wait_all(bwd_s, a2a_sem.at[4])
    wait_all(bwd_r, a2a_sem.at[5])
    returned = bwd_r[...].astype(F32).reshape(SLOTS, 2 * HD).astype(BF16)
    own_kvg[...] = dot_nn(place_back, returned).astype(BF16)

    def ag_copy(side, step, c):
        at = pl.ds(c * size, size)
        if side == 0:
            source = own_kvg.at[at] if step == 0 else ag_a.at[step - 1, at]
            return hop(source, ag_a.at[step, at], ga_s.at[step, c], ga_r.at[step, c], left)
        source = own_kvg.at[at] if step == 0 else ag_b.at[step - 1, at]
        return hop(source, ag_b.at[step, at], gb_s.at[step, c], gb_r.at[step, c], right)

    def ag_start(step):
        for c in range(CHUNKS):
            for side, steps in ((0, 4), (1, 3)):
                if step >= steps:
                    continue
                if step > 0:
                    ag_copy(side, step - 1, c).wait_recv()
                copy = ag_copy(side, step, c)
                copy.start()
                started.append(copy)

    ag_start(0)
    acc[...] = dot_nt(own_kvg[...], w_v[OFFSETS.index(0)])
    ag_start(1)
    for step in range(4):
        if step == 3:
            for c in range(CHUNKS):
                ag_copy(0, 3, c).wait_recv()
        elif step == 2:
            for c in range(CHUNKS):
                ag_copy(1, 2, c).wait_recv()
        grad = dot_nt(ag_a[step], w_v[OFFSETS.index(step + 1 if step < 3 else -4)])
        if step < 3:
            grad = grad + dot_nt(ag_b[step], w_v[OFFSETS.index(-step - 1)])
        if step == 3:
            vg_ref[...] = (acc[...] + grad).astype(BF16)
        else:
            acc[...] += grad
        if step + 2 < 4:
            ag_start(step + 2)
    for copy in started:
        copy.wait_send()


def tag_s_view(ref):
    return ref


def on_device(
    queries, text_kv, out_grad, text_segment, visual_rows, kv_weight, visual_dest, visual_sample
):
    hbm = pl.BlockSpec(memory_space=pl.ANY)
    vmem = pl.BlockSpec(memory_space=pltpu.VMEM)
    sem = pltpu.SemaphoreType.DMA
    block = (ROWS, 2 * HD)
    n_blocks = PACK // BLK
    return pl.pallas_call(
        kernel,
        out_shape=(
            jax.ShapeDtypeStruct((PACK, QPK * HD), BF16),
            jax.ShapeDtypeStruct((PACK, QPK * HD), BF16),
            jax.ShapeDtypeStruct((PACK, 2 * HD), BF16),
            jax.ShapeDtypeStruct((ROWS, kv_weight.shape[0]), BF16),
        ),
        in_specs=[hbm, hbm, hbm, vmem, hbm, hbm, vmem, vmem],
        out_specs=(vmem, vmem, vmem, vmem),
        scratch_shapes=[
            pltpu.VMEM((NZ, kv_weight.shape[0], 2 * HD), BF16),
            pltpu.VMEM(visual_rows.shape, BF16),
            pltpu.VMEM(queries.shape, BF16),
            pltpu.VMEM(text_kv.shape, BF16),
            pltpu.VMEM(out_grad.shape, BF16),
            pltpu.VMEM((NZ,) + block, F32),
            pltpu.VMEM((4,) + block, BF16),
            pltpu.VMEM((4,) + block, BF16),
            pltpu.VMEM((3,) + block, BF16),
            pltpu.VMEM((3,) + block, BF16),
            pltpu.VMEM((1, 1, NG), F32),
            pltpu.VMEM((NG, 1, NG), F32),
            pltpu.VMEM((NG, 2, 2 * HD), BF16),
            pltpu.VMEM((NG, 2, 2 * HD), BF16),
            pltpu.VMEM((NG, 2, 2 * HD), BF16),
            pltpu.VMEM((NG, 2, 2 * HD), BF16),
            pltpu.VMEM(block, BF16),
            pltpu.VMEM((4,) + block, BF16),
            pltpu.VMEM((3,) + block, BF16),
            pltpu.VMEM((ROWS, kv_weight.shape[0]), F32),
            pltpu.VMEM((n_blocks, 2 * BLK, BLK), F32),
            pltpu.VMEM((SLOTS, PACK), F32),
            pltpu.VMEM((QPK, n_blocks, 2 * BLK, BLK), F32),
            pltpu.VMEM((QPK, n_blocks, 2 * BLK, BLK), F32),
            pltpu.VMEM((QPK, 8, PACK), F32),
            pltpu.VMEM((QPK, SLOTS, PACK), BF16),
            pltpu.VMEM((QPK, SLOTS, PACK), BF16),
            pltpu.VMEM((SLOTS, 2 * HD), BF16),
            pltpu.VMEM((SLOTS, 2 * HD), F32),
            pltpu.VMEM((PACK, HD), F32),
            pltpu.VMEM((PACK, HD), F32),
            sem((NZ,)),
            sem((4,)),
            sem((4, CHUNKS)),
            sem((4, CHUNKS)),
            sem((3, CHUNKS)),
            sem((3, CHUNKS)),
            sem((6,)),
            sem((2,)),
            sem((4, CHUNKS)),
            sem((4, CHUNKS)),
            sem((3, CHUNKS)),
            sem((3, CHUNKS)),
        ],
        compiler_params=pltpu.CompilerParams(
            collective_id=0, has_side_effects=True, vmem_limit_bytes=48 << 20
        ),
        cost_estimate=pl.CostEstimate(flops=3 << 30, bytes_accessed=8 << 20, transcendentals=1 << 20),
    )(
        queries, text_kv, out_grad, text_segment, visual_rows, kv_weight,
        visual_dest.reshape(1, ROWS), visual_sample.reshape(1, ROWS),
    )


def solution(mesh):
    placed = (
        P("group", "tensor"),
        P("group", "tensor"),
        P("group", "tensor"),
        P("group", None),
        P("group", "tensor"),
        P("tensor", None),
        P("group", None),
        P("group"),
    )
    return jax.shard_map(
        on_device,
        mesh=mesh,
        in_specs=placed,
        out_specs=(P("group", "tensor"),) * 4,
        check_vma=False,
    )
```

```python
import functools
import math

import jax
import jax.numpy as jnp
from jax import lax
from jax.experimental import pallas as pl
from jax.experimental.pallas import tpu as pltpu
from jax.sharding import PartitionSpec as P

MESH = pl.DeviceIdType.MESH
HD = 128
QPK = 4
PACK = 384
BLK = 128
NZ = 8
NG = 128
ROWS = 128
SLOTS = 256
CHUNKS = 2
AROUND = (4, 3, 5, 2, 6, 1, 7, 0)
OFFSETS = (-4, 3, -3, 2, -2, 1, -1, 0)
SCALE = 1.0 / math.sqrt(HD)
F32 = jnp.float32
BF16 = jnp.bfloat16


def dot_nn(a, b):
    return lax.dot_general(a, b, (((1,), (0,)), ((), ())), preferred_element_type=F32)


def dot_nt(a, b):
    return lax.dot_general(a, b, (((1,), (1,)), ((), ())), preferred_element_type=F32)


def dot_tn(a, b):
    return lax.dot_general(a, b, (((0,), (0,)), ((), ())), preferred_element_type=F32)


def iota(shape, dim):
    return lax.broadcasted_iota(jnp.int32, shape, dim)


def column_of(row):
    n = row.shape[1]
    eye = iota((n, n), 0) == iota((n, n), 1)
    return jnp.sum(jnp.where(eye, row, 0.0), axis=1, keepdims=True)


def key_range(block):
    low = max(0, (block - 1) * BLK)
    return low, (block + 1) * BLK - low


def kernel(
    q_hbm, kv_hbm, og_hbm, seg_hbm, rows_hbm, w_hbm, dest_hbm, sample_hbm,
    att_ref, qg_ref, tg_ref, vg_ref,
    w_v, rows_v, q_v, kv_v, og_v, seg_v, dest_v, sample_v,
    part, send_a, recv_a, send_b, recv_b,
    tag_s, tag_r, fwd_s, fwd_r, bwd_s, bwd_r,
    own_kvg, ag_a, ag_b, acc,
    tmask, vmask, exp_t, dp_t, stats, p_vis, ds_vis, kv_vis, dkv_vis, dk_t, dv_t,
    w_sem, in_sem, sa_sem, ra_sem, sb_sem, rb_sem,
    a2a_sem, self_sem, news, ga_s, ga_r, gb_s, gb_r,
):
    g = lax.axis_index("group")
    t = lax.axis_index("tensor")
    gx, gy, gc = g // 16, (g // 2) % 8, g % 2
    way = 1 - 2 * gc
    left, right = (t - way + NZ) % NZ, (t + way + NZ) % NZ

    plane = [((gy + dy) % 8) * 2 + (gc + dc) % 2 for dy in AROUND for dc in (1, 0)]

    def each_peer(act):
        def one_x(k, carry):
            dx = 4 + (1 - 2 * (k % 2)) * ((k + 1) // 2)
            base = ((gx + dx) % 8) * 16
            for rest in plane:
                act(base + rest)
            return carry

        lax.fori_loop(0, 7, one_x, 0)
        for rest in plane[:-1]:
            act(gx * 16 + rest)

    def at(dx, dy, dc):
        return ((gx + dx + 8) % 8) * 16 + ((gy + dy + 8) % 8) * 2 + (gc + dc) % 2

    barrier = pltpu.get_barrier_semaphore()
    for p in (at(1, 0, 0), at(-1, 0, 0), at(0, 1, 0), at(0, -1, 0), at(0, 0, 1)):
        pl.semaphore_signal(barrier, inc=1, device_id={"group": p}, device_id_type=MESH)
    for near in (left, right):
        pl.semaphore_signal(barrier, inc=1, device_id={"tensor": near}, device_id_type=MESH)

    news_to = (
        (at(1, 0, 0), at(-1, 0, 0)),
        (at(2, 0, 0), at(-2, 0, 0)),
        (at(0, 1, 0), at(0, -1, 0)),
        (at(0, 1, 0), at(0, -1, 0)),
        (at(0, 2, 0), at(0, -2, 0)),
        (at(0, 0, 1),),
    )

    def tell(level):
        for p in news_to[level]:
            pl.semaphore_signal(news.at[level], inc=1, device_id={"group": p}, device_id_type=MESH)

    def hear(level):
        pl.semaphore_wait(news.at[level], len(news_to[level]))

    rows_in = pltpu.make_async_copy(rows_hbm, rows_v, in_sem.at[0])
    rows_in.start()
    w_in = []
    for i, off in enumerate(OFFSETS):
        column = pl.multiple_of(((t + way * off + NZ) % NZ) * 2 * HD, 2 * HD)
        copy = pltpu.make_async_copy(w_hbm.at[:, pl.ds(column, 2 * HD)], w_v.at[i], w_sem.at[i])
        copy.start()
        w_in.append(copy)
    small_in = [
        pltpu.make_async_copy(dest_hbm, dest_v, in_sem.at[4]),
        pltpu.make_async_copy(sample_hbm, sample_v, in_sem.at[5]),
        pltpu.make_async_copy(seg_hbm, seg_v, in_sem.at[6]),
    ]
    for copy in small_in:
        copy.start()
    other_in = [
        pltpu.make_async_copy(kv_hbm, kv_v, in_sem.at[1]),
        pltpu.make_async_copy(q_hbm, q_v, in_sem.at[2]),
        pltpu.make_async_copy(og_hbm, og_v, in_sem.at[3]),
    ]
    for copy in other_in:
        copy.start()

    rows_in.wait()

    def first_matmul(i):
        w_in[i].wait()
        part[i] = dot_nn(rows_v[...], w_v[i])

    size = ROWS // CHUNKS

    def hop(src, dst, ssem, rsem, near):
        return pltpu.make_async_remote_copy(
            src_ref=src, dst_ref=dst, send_sem=ssem, recv_sem=rsem,
            device_id={"tensor": near}, device_id_type=MESH,
        )

    def rs_copy(side, step, c):
        at = pl.ds(c * size, size)
        if side == 0:
            return hop(send_a.at[step, at], recv_a.at[step, at], sa_sem.at[step, c], ra_sem.at[step, c], left)
        return hop(send_b.at[step, at], recv_b.at[step, at], sb_sem.at[step, c], rb_sem.at[step, c], right)

    sides = ((0, 4, send_a, recv_a), (1, 3, send_b, recv_b))
    started = []

    def rs_step(step):
        for c in range(CHUNKS):
            lo, hi = c * size, (c + 1) * size
            for side, steps, send, recv in sides:
                if step >= steps:
                    continue
                off = step - 4 if side == 0 else 3 - step
                value = part[OFFSETS.index(off), lo:hi, :]
                if step > 0:
                    rs_copy(side, step - 1, c).wait_recv()
                    value = value + recv[step - 1, lo:hi, :].astype(F32)
                send[step, lo:hi, :] = value.astype(BF16)
                copy = rs_copy(side, step, c)
                copy.start()
                started.append(copy)

    def send_all(source, landing, ssem, rsem):
        def act(p):
            pltpu.make_async_remote_copy(
                src_ref=source(p), dst_ref=landing.at[g], send_sem=ssem, recv_sem=rsem,
                device_id={"group": p}, device_id_type=MESH,
            ).start()

        each_peer(act)

    def wait_all(buffer, sem):
        view = buffer.at[pl.ds(0, NG - 1)]
        pltpu.make_async_copy(view, view, sem).wait()

    def text_head(h):
        for block in range(PACK // BLK):
            low, n = key_range(block)
            tok = slice(block * BLK, (block + 1) * BLK)
            lanes = slice(h * HD, (h + 1) * HD)
            scores = dot_nt(kv_v[low : low + n, 0:HD], q_v[tok, lanes]) * SCALE
            scores = jnp.where(tmask[block, 0:n, :] > 0.5, scores, -jnp.inf)
            top = jnp.max(scores, axis=0, keepdims=True)
            expo = jnp.exp(scores - top)
            dprobs = dot_nt(kv_v[low : low + n, HD : 2 * HD], og_v[tok, lanes])
            exp_t[h, block, 0:n, :] = expo
            dp_t[h, block, 0:n, :] = dprobs
            stats[h, 0:1, tok] = top
            stats[h, 1:2, tok] = jnp.sum(expo, axis=0, keepdims=True)
            stats[h, 2:3, tok] = jnp.sum(expo * dprobs, axis=0, keepdims=True)

    first_matmul(0)
    first_matmul(1)
    pl.semaphore_wait(barrier, 7)
    rs_step(0)
    tell(0)
    for i in range(2, len(OFFSETS)):
        first_matmul(i)
    hear(0)
    tell(1)
    for copy in small_in:
        copy.wait()
    dest_row = dest_v[...].astype(F32)
    dest_col = column_of(dest_row)
    sample_col = column_of(sample_v[...].astype(F32))
    pack_row = iota((ROWS, NG), 1).astype(F32)
    tag_s[0] = jnp.max(
        jnp.where(dest_col == pack_row, sample_col, -1.0), axis=0, keepdims=True
    )
    parity_row = (iota((1, ROWS), 1) % 2).astype(F32)
    place_out = (iota((SLOTS, ROWS), 0).astype(F32) == dest_row * 2.0 + parity_row).astype(BF16)
    parity_col = (iota((ROWS, 1), 0) % 2).astype(F32)
    place_back = (iota((ROWS, SLOTS), 1).astype(F32) == dest_col * 2.0 + parity_col).astype(BF16)

    seg_row = seg_v[...].astype(F32)
    for block in range(PACK // BLK):
        low, n = key_range(block)
        seg_key = column_of(seg_row[:, low : low + n])
        seg_tok = seg_row[:, block * BLK : (block + 1) * BLK]
        before = iota((n, BLK), 0) + low <= iota((n, BLK), 1) + block * BLK
        tmask[block, 0:n, :] = jnp.where((seg_key == seg_tok) & before, 1.0, 0.0)

    rs_step(1)
    hear(1)
    tell(2)
    for copy in other_in:
        copy.wait()
    text_head(0)
    hear(2)
    tell(3)
    text_head(1)
    rs_step(2)
    hear(3)
    tell(4)
    text_head(2)
    hear(4)
    tell(5)
    rs_step(3)
    text_head(3)
    hear(5)
    send_all(lambda p: tag_s.at[0], tag_r, a2a_sem.at[0], a2a_sem.at[1])
    tag_r[g] = tag_s[0]

    for c in range(CHUNKS):
        rs_copy(0, 3, c).wait_recv()
        rs_copy(1, 2, c).wait_recv()
    own = (part[OFFSETS.index(0)] + recv_a[3].astype(F32)) + recv_b[2].astype(F32)
    fwd_s[...] = dot_nn(place_out, own.astype(BF16)).reshape(NG, 2, 2 * HD).astype(BF16)
    to_self = pltpu.make_async_copy(fwd_s.at[g], fwd_r.at[g], self_sem.at[0])
    to_self.start()
    send_all(lambda p: fwd_s.at[p], fwd_r, a2a_sem.at[2], a2a_sem.at[3])

    wait_all(tag_r, a2a_sem.at[0])
    wait_all(tag_r, a2a_sem.at[1])
    table = tag_r[...].reshape(NG, NG).astype(BF16)
    spread = (iota((SLOTS, NG), 0) // 2 == iota((SLOTS, NG), 1)).astype(BF16)
    by_slot = dot_nn(spread, table).astype(BF16)
    mine = (iota((NG, PACK), 0) == g).astype(BF16)
    vmask[...] = jnp.where(dot_nn(by_slot, mine) == seg_row, 1.0, 0.0)

    to_self.wait()
    wait_all(fwd_s, a2a_sem.at[2])
    wait_all(fwd_r, a2a_sem.at[3])

    kv_vis[...] = fwd_r[...].astype(F32).reshape(SLOTS, 2 * HD).astype(BF16)
    for h in range(QPK):
        lanes = slice(h * HD, (h + 1) * HD)
        q_h, og_h = q_v[:, lanes], og_v[:, lanes]
        scores = dot_nt(kv_vis[:, 0:HD], q_h) * SCALE
        scores = jnp.where(vmask[...] > 0.5, scores, -jnp.inf)
        top_t = stats[h, 0:1, :]
        top = jnp.maximum(jnp.max(scores, axis=0, keepdims=True), top_t)
        expo = jnp.exp(scores - top)
        again = jnp.exp(top_t - top)
        dprobs = dot_nt(kv_vis[:, HD : 2 * HD], og_h)
        total = stats[h, 1:2, :] * again + jnp.sum(expo, axis=0, keepdims=True)
        over = 1.0 / total
        inner = (stats[h, 2:3, :] * again + jnp.sum(expo * dprobs, axis=0, keepdims=True)) * over
        probs = expo * over
        weights = probs.astype(BF16)
        dscores = (probs * (dprobs - inner) * SCALE).astype(BF16)
        p_vis[h] = weights
        ds_vis[h] = dscores
        stats[h, 3:4, :] = again * over
        stats[h, 4:5, :] = inner
        dk = dot_nn(dscores, q_h)
        dv = dot_nn(weights, og_h)
        if h == 0:
            dkv_vis[:, 0:HD] = dk
            dkv_vis[:, HD : 2 * HD] = dv
        else:
            dkv_vis[:, 0:HD] += dk
            dkv_vis[:, HD : 2 * HD] += dv

    bwd_s[...] = dkv_vis[...].reshape(NG, 2, 2 * HD).astype(BF16)
    to_self = pltpu.make_async_copy(bwd_s.at[g], bwd_r.at[g], self_sem.at[1])
    to_self.start()
    send_all(lambda p: bwd_s.at[p], bwd_r, a2a_sem.at[4], a2a_sem.at[5])

    dk_t[...] = jnp.zeros_like(dk_t)
    dv_t[...] = jnp.zeros_like(dv_t)
    for h in range(QPK):
        for block in range(PACK // BLK):
            low, n = key_range(block)
            tok = slice(block * BLK, (block + 1) * BLK)
            lanes = slice(h * HD, (h + 1) * HD)
            probs = exp_t[h, block, 0:n, :] * stats[h, 3:4, tok]
            weights = probs.astype(BF16)
            dscores = (probs * (dp_t[h, block, 0:n, :] - stats[h, 4:5, tok]) * SCALE).astype(BF16)
            dk_t[low : low + n, :] += dot_nn(dscores, q_v[tok, lanes])
            dv_t[low : low + n, :] += dot_nn(weights, og_v[tok, lanes])
            out = dot_tn(weights, kv_v[low : low + n, HD : 2 * HD])
            out = out + dot_tn(p_vis[h, :, tok], kv_vis[:, HD : 2 * HD])
            att_ref[tok, lanes] = out.astype(BF16)
            dq = dot_tn(dscores, kv_v[low : low + n, 0:HD])
            dq = dq + dot_tn(ds_vis[h, :, tok], kv_vis[:, 0:HD])
            qg_ref[tok, lanes] = dq.astype(BF16)
    tg_ref[:, 0:HD] = dk_t[...].astype(BF16)
    tg_ref[:, HD : 2 * HD] = dv_t[...].astype(BF16)

    to_self.wait()
    wait_all(bwd_s, a2a_sem.at[4])
    wait_all(bwd_r, a2a_sem.at[5])
    returned = bwd_r[...].astype(F32).reshape(SLOTS, 2 * HD).astype(BF16)
    own_kvg[...] = dot_nn(place_back, returned).astype(BF16)

    def ag_copy(side, step, c):
        at = pl.ds(c * size, size)
        if side == 0:
            source = own_kvg.at[at] if step == 0 else ag_a.at[step - 1, at]
            return hop(source, ag_a.at[step, at], ga_s.at[step, c], ga_r.at[step, c], left)
        source = own_kvg.at[at] if step == 0 else ag_b.at[step - 1, at]
        return hop(source, ag_b.at[step, at], gb_s.at[step, c], gb_r.at[step, c], right)

    def ag_start(step):
        for c in range(CHUNKS):
            for side, steps in ((0, 4), (1, 3)):
                if step >= steps:
                    continue
                if step > 0:
                    ag_copy(side, step - 1, c).wait_recv()
                copy = ag_copy(side, step, c)
                copy.start()
                started.append(copy)

    ag_start(0)
    acc[...] = dot_nt(own_kvg[...], w_v[OFFSETS.index(0)])
    ag_start(1)
    for step in range(4):
        if step == 3:
            for c in range(CHUNKS):
                ag_copy(0, 3, c).wait_recv()
        elif step == 2:
            for c in range(CHUNKS):
                ag_copy(1, 2, c).wait_recv()
        grad = dot_nt(ag_a[step], w_v[OFFSETS.index(step + 1 if step < 3 else -4)])
        if step < 3:
            grad = grad + dot_nt(ag_b[step], w_v[OFFSETS.index(-step - 1)])
        if step == 3:
            vg_ref[...] = (acc[...] + grad).astype(BF16)
        else:
            acc[...] += grad
        if step + 2 < 4:
            ag_start(step + 2)
    for copy in started:
        copy.wait_send()


def write_out(*refs):
    sems = refs[8]
    copies = [pltpu.make_async_copy(refs[i], refs[4 + i], sems.at[i]) for i in range(4)]
    for copy in copies:
        copy.start()
    for copy in copies:
        copy.wait()


def on_device(
    queries, text_kv, out_grad, text_segment, visual_rows, kv_weight, visual_dest, visual_sample
):
    hbm = pl.BlockSpec(memory_space=pltpu.HBM)
    vmem = pl.BlockSpec(memory_space=pltpu.VMEM)
    sem = pltpu.SemaphoreType.DMA
    block = (ROWS, 2 * HD)
    n_blocks = PACK // BLK
    results = pl.pallas_call(
        kernel,
        out_shape=(
            jax.ShapeDtypeStruct((PACK, QPK * HD), BF16),
            jax.ShapeDtypeStruct((PACK, QPK * HD), BF16),
            jax.ShapeDtypeStruct((PACK, 2 * HD), BF16),
            jax.ShapeDtypeStruct((ROWS, kv_weight.shape[0]), BF16),
        ),
        in_specs=[hbm] * 8,
        out_specs=(vmem, vmem, vmem, vmem),
        scratch_shapes=[
            pltpu.VMEM((NZ, kv_weight.shape[0], 2 * HD), BF16),
            pltpu.VMEM(visual_rows.shape, BF16),
            pltpu.VMEM(queries.shape, BF16),
            pltpu.VMEM(text_kv.shape, BF16),
            pltpu.VMEM(out_grad.shape, BF16),
            pltpu.VMEM(text_segment.shape, jnp.int32),
            pltpu.VMEM((1, ROWS), jnp.int32),
            pltpu.VMEM((1, ROWS), jnp.int32),
            pltpu.VMEM((NZ,) + block, F32),
            pltpu.VMEM((4,) + block, BF16),
            pltpu.VMEM((4,) + block, BF16),
            pltpu.VMEM((3,) + block, BF16),
            pltpu.VMEM((3,) + block, BF16),
            pltpu.VMEM((1, 1, NG), F32),
            pltpu.VMEM((NG, 1, NG), F32),
            pltpu.VMEM((NG, 2, 2 * HD), BF16),
            pltpu.VMEM((NG, 2, 2 * HD), BF16),
            pltpu.VMEM((NG, 2, 2 * HD), BF16),
            pltpu.VMEM((NG, 2, 2 * HD), BF16),
            pltpu.VMEM(block, BF16),
            pltpu.VMEM((4,) + block, BF16),
            pltpu.VMEM((3,) + block, BF16),
            pltpu.VMEM((ROWS, kv_weight.shape[0]), F32),
            pltpu.VMEM((n_blocks, 2 * BLK, BLK), F32),
            pltpu.VMEM((SLOTS, PACK), F32),
            pltpu.VMEM((QPK, n_blocks, 2 * BLK, BLK), F32),
            pltpu.VMEM((QPK, n_blocks, 2 * BLK, BLK), F32),
            pltpu.VMEM((QPK, 8, PACK), F32),
            pltpu.VMEM((QPK, SLOTS, PACK), BF16),
            pltpu.VMEM((QPK, SLOTS, PACK), BF16),
            pltpu.VMEM((SLOTS, 2 * HD), BF16),
            pltpu.VMEM((SLOTS, 2 * HD), F32),
            pltpu.VMEM((PACK, HD), F32),
            pltpu.VMEM((PACK, HD), F32),
            sem((NZ,)),
            sem((7,)),
            sem((4, CHUNKS)),
            sem((4, CHUNKS)),
            sem((3, CHUNKS)),
            sem((3, CHUNKS)),
            sem((6,)),
            sem((2,)),
            pltpu.SemaphoreType.REGULAR((6,)),
            sem((4, CHUNKS)),
            sem((4, CHUNKS)),
            sem((3, CHUNKS)),
            sem((3, CHUNKS)),
        ],
        compiler_params=pltpu.CompilerParams(
            collective_id=0, has_side_effects=True, vmem_limit_bytes=48 << 20
        ),
        cost_estimate=pl.CostEstimate(flops=3 << 30, bytes_accessed=8 << 20, transcendentals=1 << 20),
    )(
        *(
            pltpu.with_memory_space_constraint(x, pltpu.HBM)
            for x in (
                queries, text_kv, out_grad, text_segment, visual_rows, kv_weight,
                visual_dest.reshape(1, ROWS), visual_sample.reshape(1, ROWS),
            )
        )
    )
    return pl.pallas_call(
        write_out,
        out_shape=tuple(jax.ShapeDtypeStruct(r.shape, r.dtype) for r in results),
        in_specs=[vmem] * 4,
        out_specs=(hbm,) * 4,
        scratch_shapes=[sem((4,))],
        cost_estimate=pl.CostEstimate(flops=0, bytes_accessed=2 << 20, transcendentals=0),
    )(*(pltpu.with_memory_space_constraint(r, pltpu.VMEM) for r in results))


def solution(mesh):
    placed = (
        P("group", "tensor"),
        P("group", "tensor"),
        P("group", "tensor"),
        P("group", None),
        P("group", "tensor"),
        P("tensor", None),
        P("group", None),
        P("group"),
    )
    return jax.shard_map(
        on_device,
        mesh=mesh,
        in_specs=placed,
        out_specs=(P("group", "tensor"),) * 4,
        check_vma=False,
    )
```

```python
import functools
import math

import jax
import jax.numpy as jnp
from jax import lax
from jax.experimental import pallas as pl
from jax.experimental.pallas import tpu as pltpu
from jax.sharding import PartitionSpec as P

MESH = pl.DeviceIdType.MESH
HD = 128
QPK = 4
PACK = 384
BLK = 128
NZ = 8
NG = 128
ROWS = 128
SLOTS = 256
CHUNKS = 2
FIRST = 3
AROUND = (4, 3, 5, 2, 6, 1, 7, 0)
OFFSETS = (-4, 3, -3, -2, 2, -1, 1, 0)
SCALE = 1.0 / math.sqrt(HD)
F32 = jnp.float32
BF16 = jnp.bfloat16


def dot_nn(a, b):
    return lax.dot_general(a, b, (((1,), (0,)), ((), ())), preferred_element_type=F32)


def dot_nt(a, b):
    return lax.dot_general(a, b, (((1,), (1,)), ((), ())), preferred_element_type=F32)


def dot_tn(a, b):
    return lax.dot_general(a, b, (((0,), (0,)), ((), ())), preferred_element_type=F32)


def iota(shape, dim):
    return lax.broadcasted_iota(jnp.int32, shape, dim)


def column_of(row):
    n = row.shape[1]
    eye = iota((n, n), 0) == iota((n, n), 1)
    return jnp.sum(jnp.where(eye, row, 0.0), axis=1, keepdims=True)


def key_range(block):
    low = max(0, (block - 1) * BLK)
    return low, (block + 1) * BLK - low


def kernel(
    q_hbm, kv_hbm, og_hbm, seg_hbm, rows_hbm, w_hbm, dest_hbm, sample_hbm,
    att_ref, qg_ref, tg_ref, vg_ref,
    w_v, rows_v, q_v, kv_v, og_v, seg_v, dest_v, sample_v,
    part, send_a, recv_a, send_b, recv_b,
    tag_x, tag_r, fwd_s, fwd_r, bwd_s, bwd_r,
    own_kvg, ag_a, ag_b, acc,
    tmask, vmask, exp_t, dp_t, stats, p_vis, ds_vis, kv_vis, dkv_vis, dk_t, dv_t,
    w_sem, in_sem, sa_sem, ra_sem, sb_sem, rb_sem,
    a2a_sem, self_sem, news, ga_s, ga_r, gb_s, gb_r,
):
    g = lax.axis_index("group")
    t = lax.axis_index("tensor")
    gx, gy, gc = g // 16, (g // 2) % 8, g % 2
    way = 1 - 2 * gc
    left, right = (t - way + NZ) % NZ, (t + way + NZ) % NZ
    left2, right2 = (t - 2 * way + NZ) % NZ, (t + 2 * way + NZ) % NZ

    plane = [((gy + dy) % 8) * 2 + (gc + dc) % 2 for dy in AROUND for dc in (1, 0)]

    def each_peer(act):
        def one_x(k, carry):
            dx = 4 + (1 - 2 * (k % 2)) * ((k + 1) // 2)
            base = ((gx + dx) % 8) * 16
            for rest in plane:
                act(base + rest)
            return carry

        lax.fori_loop(0, 7, one_x, 0)
        for rest in plane[:-1]:
            act(gx * 16 + rest)

    def at(dx, dy, dc):
        return ((gx + dx + 8) % 8) * 16 + ((gy + dy + 8) % 8) * 2 + (gc + dc) % 2

    barrier = pltpu.get_barrier_semaphore()
    for p in (at(1, 0, 0), at(-1, 0, 0), at(0, 1, 0), at(0, -1, 0), at(0, 0, 1)):
        pl.semaphore_signal(barrier, inc=1, device_id={"group": p}, device_id_type=MESH)
    for near in (left, right, left2, right2):
        pl.semaphore_signal(barrier, inc=1, device_id={"tensor": near}, device_id_type=MESH)

    news_to = (
        (at(1, 0, 0), at(-1, 0, 0)),
        (at(2, 0, 0), at(-2, 0, 0)),
        (at(0, 1, 0), at(0, -1, 0)),
        (at(0, 1, 0), at(0, -1, 0)),
        (at(0, 2, 0), at(0, -2, 0)),
        (at(0, 0, 1),),
    )

    def tell(level):
        for p in news_to[level]:
            pl.semaphore_signal(news.at[level], inc=1, device_id={"group": p}, device_id_type=MESH)

    def hear(level):
        pl.semaphore_wait(news.at[level], len(news_to[level]))

    rows_in = pltpu.make_async_copy(rows_hbm, rows_v, in_sem.at[0])
    rows_in.start()
    w_in = []
    for i, off in enumerate(OFFSETS):
        column = pl.multiple_of(((t + way * off + NZ) % NZ) * 2 * HD, 2 * HD)
        copy = pltpu.make_async_copy(w_hbm.at[:, pl.ds(column, 2 * HD)], w_v.at[i], w_sem.at[i])
        if i < FIRST:
            copy.start()
        w_in.append(copy)
    small_in = [
        pltpu.make_async_copy(dest_hbm, dest_v, in_sem.at[4]),
        pltpu.make_async_copy(sample_hbm, sample_v, in_sem.at[5]),
        pltpu.make_async_copy(seg_hbm, seg_v, in_sem.at[6]),
    ]
    other_in = [
        pltpu.make_async_copy(kv_hbm, kv_v, in_sem.at[1]),
        pltpu.make_async_copy(q_hbm, q_v, in_sem.at[2]),
        pltpu.make_async_copy(og_hbm, og_v, in_sem.at[3]),
    ]
    rows_in.wait()

    def first_matmul(i):
        w_in[i].wait()
        part[i] = dot_nn(rows_v[...], w_v[i])

    size = ROWS // CHUNKS

    def hop(src, dst, ssem, rsem, near):
        return pltpu.make_async_remote_copy(
            src_ref=src, dst_ref=dst, send_sem=ssem, recv_sem=rsem,
            device_id={"tensor": near}, device_id_type=MESH,
        )

    legs = {
        (0, 0): (-4, left2), (0, 1): (-3, left), (0, 2): (-1, left), (0, 3): (-2, left2),
        (1, 0): (3, right), (1, 1): (1, right), (1, 2): (2, right2),
    }
    started = []

    def rs_copy(side, place, c):
        part_of = pl.ds(c * size, size)
        near = legs[side, place][1]
        if side == 0:
            return hop(send_a.at[place, part_of], recv_a.at[place, part_of], sa_sem.at[place, c], ra_sem.at[place, c], near)
        return hop(send_b.at[place, part_of], recv_b.at[place, part_of], sb_sem.at[place, c], rb_sem.at[place, c], near)

    def rs_send(side, place, with_places=()):
        send, recv = (send_a, recv_a) if side == 0 else (send_b, recv_b)
        for c in range(CHUNKS):
            lo, hi = c * size, (c + 1) * size
            value = part[OFFSETS.index(legs[side, place][0]), lo:hi, :]
            for other in with_places:
                rs_copy(side, other, c).wait_recv()
                value = value + recv[other, lo:hi, :].astype(F32)
            send[place, lo:hi, :] = value.astype(BF16)
            copy = rs_copy(side, place, c)
            copy.start()
            started.append(copy)

    def send_all(source, landing, ssem, rsem):
        def act(p):
            pltpu.make_async_remote_copy(
                src_ref=source(p), dst_ref=landing.at[g], send_sem=ssem, recv_sem=rsem,
                device_id={"group": p}, device_id_type=MESH,
            ).start()

        each_peer(act)

    def wait_rows(buffer, count, sem):
        view = buffer.at[pl.ds(0, count)]
        pltpu.make_async_copy(view, view, sem).wait()

    def wait_all(buffer, sem):
        wait_rows(buffer, NG - 1, sem)

    def text_head(h):
        for block in range(PACK // BLK):
            low, n = key_range(block)
            tok = slice(block * BLK, (block + 1) * BLK)
            lanes = slice(h * HD, (h + 1) * HD)
            scores = dot_nt(kv_v[low : low + n, 0:HD], q_v[tok, lanes]) * SCALE
            scores = jnp.where(tmask[block, 0:n, :] > 0.5, scores, -jnp.inf)
            top = jnp.max(scores, axis=0, keepdims=True)
            expo = jnp.exp(scores - top)
            dprobs = dot_nt(kv_v[low : low + n, HD : 2 * HD], og_v[tok, lanes])
            exp_t[h, block, 0:n, :] = expo
            dp_t[h, block, 0:n, :] = dprobs
            stats[h, 0:1, tok] = top
            stats[h, 1:2, tok] = jnp.sum(expo, axis=0, keepdims=True)
            stats[h, 2:3, tok] = jnp.sum(expo * dprobs, axis=0, keepdims=True)

    first_matmul(0)
    for copy in w_in[FIRST:] + small_in + other_in:
        copy.start()
    pl.semaphore_wait(barrier, 9)
    tell(0)
    rs_send(0, 0)
    first_matmul(1)
    rs_send(1, 0)
    first_matmul(2)
    rs_send(0, 1)
    for i in range(3, len(OFFSETS)):
        first_matmul(i)
    rs_send(0, 2)
    rs_send(1, 1)
    hear(0)
    tell(1)
    for copy in small_in:
        copy.wait()
    dest_row = dest_v[...].astype(F32)
    dest_col = column_of(dest_row)
    sample_col = column_of(sample_v[...].astype(F32))
    pack_row = iota((ROWS, NG), 1).astype(F32)
    tag_x[gx] = jnp.max(
        jnp.where(dest_col == pack_row, sample_col, -1.0), axis=0, keepdims=True
    )
    parity_row = (iota((1, ROWS), 1) % 2).astype(F32)
    place_out = (iota((SLOTS, ROWS), 0).astype(F32) == dest_row * 2.0 + parity_row).astype(BF16)
    parity_col = (iota((ROWS, 1), 0) % 2).astype(F32)
    place_back = (iota((ROWS, SLOTS), 1).astype(F32) == dest_col * 2.0 + parity_col).astype(BF16)

    seg_row = seg_v[...].astype(F32)
    for block in range(PACK // BLK):
        low, n = key_range(block)
        seg_key = column_of(seg_row[:, low : low + n])
        seg_tok = seg_row[:, block * BLK : (block + 1) * BLK]
        before = iota((n, BLK), 0) + low <= iota((n, BLK), 1) + block * BLK
        tmask[block, 0:n, :] = jnp.where((seg_key == seg_tok) & before, 1.0, 0.0)

    hear(1)
    tell(2)
    for dx in AROUND[:-1]:
        pltpu.make_async_remote_copy(
            src_ref=tag_x.at[gx], dst_ref=tag_x.at[gx],
            send_sem=a2a_sem.at[6], recv_sem=a2a_sem.at[7],
            device_id={"group": at(dx, 0, 0)}, device_id_type=MESH,
        ).start()
    rs_send(0, 3, (0, 1))
    rs_send(1, 2, (0,))
    hear(2)
    tell(3)
    for copy in other_in:
        copy.wait()
    text_head(0)
    hear(3)
    tell(4)
    text_head(1)
    text_head(2)
    hear(4)
    tell(5)
    text_head(3)
    hear(5)
    wait_rows(tag_x, NZ - 1, a2a_sem.at[6])
    wait_rows(tag_x, NZ - 1, a2a_sem.at[7])
    ring = pl.ds((gy * 2 + gc) * 8, 8)
    for rest in plane[:-1]:
        pltpu.make_async_remote_copy(
            src_ref=tag_x, dst_ref=tag_r.at[ring],
            send_sem=a2a_sem.at[0], recv_sem=a2a_sem.at[1],
            device_id={"group": gx * 16 + rest}, device_id_type=MESH,
        ).start()
    tag_r[ring] = tag_x[...]

    own = part[OFFSETS.index(0)]
    for side, place, recv in ((0, 2, recv_a), (1, 1, recv_b), (1, 2, recv_b), (0, 3, recv_a)):
        for c in range(CHUNKS):
            rs_copy(side, place, c).wait_recv()
        own = own + recv[place].astype(F32)
    fwd_s[...] = dot_nn(place_out, own.astype(BF16)).reshape(NG, 2, 2 * HD).astype(BF16)
    to_self = pltpu.make_async_copy(fwd_s.at[g], fwd_r.at[g], self_sem.at[0])
    to_self.start()
    send_all(lambda p: fwd_s.at[p], fwd_r, a2a_sem.at[2], a2a_sem.at[3])

    wait_rows(tag_r, NG - 8, a2a_sem.at[0])
    wait_rows(tag_r, NG - 8, a2a_sem.at[1])
    table = tag_r[...].reshape(NG, NG).astype(BF16)
    source = iota((SLOTS, NG), 0) // 2
    spread = ((source % 16) * 8 + source // 16 == iota((SLOTS, NG), 1)).astype(BF16)
    by_slot = dot_nn(spread, table).astype(BF16)
    mine = (iota((NG, PACK), 0) == g).astype(BF16)
    vmask[...] = jnp.where(dot_nn(by_slot, mine) == seg_row, 1.0, 0.0)

    to_self.wait()
    wait_all(fwd_s, a2a_sem.at[2])
    wait_all(fwd_r, a2a_sem.at[3])

    kv_vis[...] = fwd_r[...].astype(F32).reshape(SLOTS, 2 * HD).astype(BF16)
    for h in range(QPK):
        lanes = slice(h * HD, (h + 1) * HD)
        q_h, og_h = q_v[:, lanes], og_v[:, lanes]
        scores = dot_nt(kv_vis[:, 0:HD], q_h) * SCALE
        scores = jnp.where(vmask[...] > 0.5, scores, -jnp.inf)
        top_t = stats[h, 0:1, :]
        top = jnp.maximum(jnp.max(scores, axis=0, keepdims=True), top_t)
        expo = jnp.exp(scores - top)
        again = jnp.exp(top_t - top)
        dprobs = dot_nt(kv_vis[:, HD : 2 * HD], og_h)
        total = stats[h, 1:2, :] * again + jnp.sum(expo, axis=0, keepdims=True)
        over = 1.0 / total
        inner = (stats[h, 2:3, :] * again + jnp.sum(expo * dprobs, axis=0, keepdims=True)) * over
        probs = expo * over
        weights = probs.astype(BF16)
        dscores = (probs * (dprobs - inner) * SCALE).astype(BF16)
        p_vis[h] = weights
        ds_vis[h] = dscores
        stats[h, 3:4, :] = again * over
        stats[h, 4:5, :] = inner
        dk = dot_nn(dscores, q_h)
        dv = dot_nn(weights, og_h)
        if h == 0:
            dkv_vis[:, 0:HD] = dk
            dkv_vis[:, HD : 2 * HD] = dv
        else:
            dkv_vis[:, 0:HD] += dk
            dkv_vis[:, HD : 2 * HD] += dv

    bwd_s[...] = dkv_vis[...].reshape(NG, 2, 2 * HD).astype(BF16)
    to_self = pltpu.make_async_copy(bwd_s.at[g], bwd_r.at[g], self_sem.at[1])
    to_self.start()
    send_all(lambda p: bwd_s.at[p], bwd_r, a2a_sem.at[4], a2a_sem.at[5])

    dk_t[...] = jnp.zeros_like(dk_t)
    dv_t[...] = jnp.zeros_like(dv_t)
    for h in range(QPK):
        for block in range(PACK // BLK):
            low, n = key_range(block)
            tok = slice(block * BLK, (block + 1) * BLK)
            lanes = slice(h * HD, (h + 1) * HD)
            probs = exp_t[h, block, 0:n, :] * stats[h, 3:4, tok]
            weights = probs.astype(BF16)
            dscores = (probs * (dp_t[h, block, 0:n, :] - stats[h, 4:5, tok]) * SCALE).astype(BF16)
            dk_t[low : low + n, :] += dot_nn(dscores, q_v[tok, lanes])
            dv_t[low : low + n, :] += dot_nn(weights, og_v[tok, lanes])
            out = dot_tn(weights, kv_v[low : low + n, HD : 2 * HD])
            out = out + dot_tn(p_vis[h, :, tok], kv_vis[:, HD : 2 * HD])
            att_ref[tok, lanes] = out.astype(BF16)
            dq = dot_tn(dscores, kv_v[low : low + n, 0:HD])
            dq = dq + dot_tn(ds_vis[h, :, tok], kv_vis[:, 0:HD])
            qg_ref[tok, lanes] = dq.astype(BF16)
    tg_ref[:, 0:HD] = dk_t[...].astype(BF16)
    tg_ref[:, HD : 2 * HD] = dv_t[...].astype(BF16)

    to_self.wait()
    wait_all(bwd_s, a2a_sem.at[4])
    wait_all(bwd_r, a2a_sem.at[5])
    returned = bwd_r[...].astype(F32).reshape(SLOTS, 2 * HD).astype(BF16)
    own_kvg[...] = dot_nn(place_back, returned).astype(BF16)

    def ag_copy(side, place, c):
        part_of = pl.ds(c * size, size)
        if side == 0:
            source = own_kvg.at[part_of] if place < 2 else ag_a.at[1, part_of]
            near = left2 if place % 2 == 1 else left
            return hop(source, ag_a.at[place, part_of], ga_s.at[place, c], ga_r.at[place, c], near)
        source = own_kvg.at[part_of] if place < 2 else ag_b.at[1, part_of]
        near = right2 if place == 1 else right
        return hop(source, ag_b.at[place, part_of], gb_s.at[place, c], gb_r.at[place, c], near)

    def ag_start(*which):
        for c in range(CHUNKS):
            for side, place in which:
                if place == 3 or (side, place) == (1, 2):
                    ag_copy(side, 1, c).wait_recv()
                copy = ag_copy(side, place, c)
                copy.start()
                started.append(copy)

    def ag_block(side, place):
        block = ag_a[place] if side == 0 else ag_b[place]
        distance = place + 1 if side == 0 else -1 - place
        return dot_nt(block, w_v[OFFSETS.index(distance if distance != 4 else -4)])

    def ag_wait(side, place):
        for c in range(CHUNKS):
            ag_copy(side, place, c).wait_recv()

    ag_start((0, 1), (1, 1))
    ag_start((0, 0), (1, 0))
    acc[...] = dot_nt(own_kvg[...], w_v[OFFSETS.index(0)])
    ag_start((0, 3), (0, 2), (1, 2))
    acc[...] += ag_block(0, 1) + ag_block(1, 1)
    ag_wait(0, 0)
    ag_wait(1, 0)
    acc[...] += ag_block(0, 0) + ag_block(1, 0)
    ag_wait(0, 2)
    ag_wait(1, 2)
    acc[...] += ag_block(0, 2) + ag_block(1, 2)
    ag_wait(0, 3)
    vg_ref[...] = (acc[...] + ag_block(0, 3)).astype(BF16)
    for copy in started:
        copy.wait_send()


def write_out(*refs):
    sems = refs[8]
    copies = [pltpu.make_async_copy(refs[i], refs[4 + i], sems.at[i]) for i in range(4)]
    for copy in copies:
        copy.start()
    for copy in copies:
        copy.wait()


def on_device(
    queries, text_kv, out_grad, text_segment, visual_rows, kv_weight, visual_dest, visual_sample
):
    hbm = pl.BlockSpec(memory_space=pltpu.HBM)
    vmem = pl.BlockSpec(memory_space=pltpu.VMEM)
    sem = pltpu.SemaphoreType.DMA
    block = (ROWS, 2 * HD)
    n_blocks = PACK // BLK
    results = pl.pallas_call(
        kernel,
        out_shape=(
            jax.ShapeDtypeStruct((PACK, QPK * HD), BF16),
            jax.ShapeDtypeStruct((PACK, QPK * HD), BF16),
            jax.ShapeDtypeStruct((PACK, 2 * HD), BF16),
            jax.ShapeDtypeStruct((ROWS, kv_weight.shape[0]), BF16),
        ),
        in_specs=[hbm] * 8,
        out_specs=(vmem, vmem, vmem, vmem),
        scratch_shapes=[
            pltpu.VMEM((NZ, kv_weight.shape[0], 2 * HD), BF16),
            pltpu.VMEM(visual_rows.shape, BF16),
            pltpu.VMEM(queries.shape, BF16),
            pltpu.VMEM(text_kv.shape, BF16),
            pltpu.VMEM(out_grad.shape, BF16),
            pltpu.VMEM(text_segment.shape, jnp.int32),
            pltpu.VMEM((1, ROWS), jnp.int32),
            pltpu.VMEM((1, ROWS), jnp.int32),
            pltpu.VMEM((NZ,) + block, F32),
            pltpu.VMEM((4,) + block, BF16),
            pltpu.VMEM((4,) + block, BF16),
            pltpu.VMEM((3,) + block, BF16),
            pltpu.VMEM((3,) + block, BF16),
            pltpu.VMEM((8, 1, NG), F32),
            pltpu.VMEM((NG, 1, NG), F32),
            pltpu.VMEM((NG, 2, 2 * HD), BF16),
            pltpu.VMEM((NG, 2, 2 * HD), BF16),
            pltpu.VMEM((NG, 2, 2 * HD), BF16),
            pltpu.VMEM((NG, 2, 2 * HD), BF16),
            pltpu.VMEM(block, BF16),
            pltpu.VMEM((4,) + block, BF16),
            pltpu.VMEM((3,) + block, BF16),
            pltpu.VMEM((ROWS, kv_weight.shape[0]), F32),
            pltpu.VMEM((n_blocks, 2 * BLK, BLK), F32),
            pltpu.VMEM((SLOTS, PACK), F32),
            pltpu.VMEM((QPK, n_blocks, 2 * BLK, BLK), F32),
            pltpu.VMEM((QPK, n_blocks, 2 * BLK, BLK), F32),
            pltpu.VMEM((QPK, 8, PACK), F32),
            pltpu.VMEM((QPK, SLOTS, PACK), BF16),
            pltpu.VMEM((QPK, SLOTS, PACK), BF16),
            pltpu.VMEM((SLOTS, 2 * HD), BF16),
            pltpu.VMEM((SLOTS, 2 * HD), F32),
            pltpu.VMEM((PACK, HD), F32),
            pltpu.VMEM((PACK, HD), F32),
            sem((NZ,)),
            sem((7,)),
            sem((4, CHUNKS)),
            sem((4, CHUNKS)),
            sem((3, CHUNKS)),
            sem((3, CHUNKS)),
            sem((8,)),
            sem((2,)),
            pltpu.SemaphoreType.REGULAR((6,)),
            sem((4, CHUNKS)),
            sem((4, CHUNKS)),
            sem((3, CHUNKS)),
            sem((3, CHUNKS)),
        ],
        compiler_params=pltpu.CompilerParams(
            collective_id=0, has_side_effects=True, vmem_limit_bytes=48 << 20
        ),
        cost_estimate=pl.CostEstimate(flops=3 << 30, bytes_accessed=8 << 20, transcendentals=1 << 20),
    )(
        *(
            pltpu.with_memory_space_constraint(x, pltpu.HBM)
            for x in (
                queries, text_kv, out_grad, text_segment, visual_rows, kv_weight,
                visual_dest.reshape(1, ROWS), visual_sample.reshape(1, ROWS),
            )
        )
    )
    return pl.pallas_call(
        write_out,
        out_shape=tuple(jax.ShapeDtypeStruct(r.shape, r.dtype) for r in results),
        in_specs=[vmem] * 4,
        out_specs=(hbm,) * 4,
        scratch_shapes=[sem((4,))],
        cost_estimate=pl.CostEstimate(flops=0, bytes_accessed=2 << 20, transcendentals=0),
    )(*(pltpu.with_memory_space_constraint(r, pltpu.VMEM) for r in results))


def solution(mesh):
    placed = (
        P("group", "tensor"),
        P("group", "tensor"),
        P("group", "tensor"),
        P("group", None),
        P("group", "tensor"),
        P("tensor", None),
        P("group", None),
        P("group"),
    )
    return jax.shard_map(
        on_device,
        mesh=mesh,
        in_specs=placed,
        out_specs=(P("group", "tensor"),) * 4,
        check_vma=False,
    )
```

```python
import functools
import math

import jax
import jax.numpy as jnp
from jax import lax
from jax.experimental import pallas as pl
from jax.experimental.pallas import tpu as pltpu
from jax.sharding import PartitionSpec as P

MESH = pl.DeviceIdType.MESH
HD = 128
QPK = 4
PACK = 384
BLK = 128
NZ = 8
NG = 128
ROWS = 128
SLOTS = 256
CHUNKS = 2
FIRST = 3
AROUND = (4, 3, 5, 2, 6, 1, 7, 0)
OFFSETS = (-4, 3, -3, -2, 2, -1, 1, 0)
SCALE = 1.0 / math.sqrt(HD)
F32 = jnp.float32
BF16 = jnp.bfloat16


def dot_nn(a, b):
    return lax.dot_general(a, b, (((1,), (0,)), ((), ())), preferred_element_type=F32)


def dot_nt(a, b):
    return lax.dot_general(a, b, (((1,), (1,)), ((), ())), preferred_element_type=F32)


def dot_tn(a, b):
    return lax.dot_general(a, b, (((0,), (0,)), ((), ())), preferred_element_type=F32)


def iota(shape, dim):
    return lax.broadcasted_iota(jnp.int32, shape, dim)


def column_of(row):
    n = row.shape[1]
    eye = iota((n, n), 0) == iota((n, n), 1)
    return jnp.sum(jnp.where(eye, row, 0.0), axis=1, keepdims=True)


def key_range(block):
    low = max(0, (block - 1) * BLK)
    return low, (block + 1) * BLK - low


def kernel(
    q_hbm, kv_hbm, og_hbm, seg_hbm, rows_hbm, w_hbm, dest_hbm, sample_hbm,
    att_ref, qg_ref, tg_ref, vg_ref,
    w_v, rows_v, q_v, kv_v, og_v, seg_v, dest_v, sample_v,
    part, send_a, recv_a, send_b, recv_b,
    tag_x, tag_r, fwd_s, fwd_r, bwd_s, bwd_r,
    own_kvg, ag_a, ag_b, acc,
    tmask, vmask, exp_t, dp_t, stats, p_vis, ds_vis, kv_vis, dkv_vis, dk_t, dv_t,
    w_sem, in_sem, sa_sem, ra_sem, sb_sem, rb_sem,
    a2a_sem, self_sem, news, ga_s, ga_r, gb_s, gb_r,
):
    g = lax.axis_index("group")
    t = lax.axis_index("tensor")
    gx, gy, gc = g // 16, (g // 2) % 8, g % 2
    way = 1 - 2 * gc
    left, right = (t - way + NZ) % NZ, (t + way + NZ) % NZ
    left2, right2 = (t - 2 * way + NZ) % NZ, (t + 2 * way + NZ) % NZ

    plane = [((gy + dy) % 8) * 2 + (gc + dc) % 2 for dy in AROUND for dc in (1, 0)]

    def each_peer(act):
        def one_x(k, carry):
            dx = 4 + (1 - 2 * (k % 2)) * ((k + 1) // 2)
            base = ((gx + dx) % 8) * 16
            for rest in plane:
                act(base + rest)
            return carry

        lax.fori_loop(0, 7, one_x, 0)
        for rest in plane[:-1]:
            act(gx * 16 + rest)

    def at(dx, dy, dc):
        return ((gx + dx + 8) % 8) * 16 + ((gy + dy + 8) % 8) * 2 + (gc + dc) % 2

    barrier = pltpu.get_barrier_semaphore()
    for p in (at(1, 0, 0), at(-1, 0, 0), at(0, 1, 0), at(0, -1, 0), at(0, 0, 1)):
        pl.semaphore_signal(barrier, inc=1, device_id={"group": p}, device_id_type=MESH)
    for near in (left, right, left2, right2):
        pl.semaphore_signal(barrier, inc=1, device_id={"tensor": near}, device_id_type=MESH)

    news_to = (
        (at(1, 0, 0), at(-1, 0, 0)),
        (at(2, 0, 0), at(-2, 0, 0)),
        (at(0, 1, 0), at(0, -1, 0)),
        (at(0, 1, 0), at(0, -1, 0)),
        (at(0, 2, 0), at(0, -2, 0)),
        (at(0, 0, 1),),
    )

    def tell(level):
        for p in news_to[level]:
            pl.semaphore_signal(news.at[level], inc=1, device_id={"group": p}, device_id_type=MESH)

    def hear(level):
        pl.semaphore_wait(news.at[level], len(news_to[level]))

    rows_in = pltpu.make_async_copy(rows_hbm, rows_v, in_sem.at[0])
    rows_in.start()
    w_in = []
    for i, off in enumerate(OFFSETS):
        column = pl.multiple_of(((t + way * off + NZ) % NZ) * 2 * HD, 2 * HD)
        copy = pltpu.make_async_copy(w_hbm.at[:, pl.ds(column, 2 * HD)], w_v.at[i], w_sem.at[i])
        if i < FIRST:
            copy.start()
        w_in.append(copy)
    small_in = [
        pltpu.make_async_copy(dest_hbm, dest_v, in_sem.at[4]),
        pltpu.make_async_copy(sample_hbm, sample_v, in_sem.at[5]),
        pltpu.make_async_copy(seg_hbm, seg_v, in_sem.at[6]),
    ]
    other_in = [
        pltpu.make_async_copy(kv_hbm, kv_v, in_sem.at[1]),
        pltpu.make_async_copy(q_hbm, q_v, in_sem.at[2]),
        pltpu.make_async_copy(og_hbm, og_v, in_sem.at[3]),
    ]
    rows_in.wait()

    def first_matmul(i):
        w_in[i].wait()
        part[i] = dot_nn(rows_v[...], w_v[i])

    size = ROWS // CHUNKS

    def hop(src, dst, ssem, rsem, near):
        return pltpu.make_async_remote_copy(
            src_ref=src, dst_ref=dst, send_sem=ssem, recv_sem=rsem,
            device_id={"tensor": near}, device_id_type=MESH,
        )

    legs = {
        (0, 0): (-4, left2), (0, 1): (-3, left), (0, 2): (-1, left), (0, 3): (-2, left2),
        (1, 0): (3, right), (1, 1): (1, right), (1, 2): (2, right2),
    }
    started = []

    def rs_copy(side, place, c):
        part_of = pl.ds(c * size, size)
        near = legs[side, place][1]
        if side == 0:
            return hop(send_a.at[place, part_of], recv_a.at[place, part_of], sa_sem.at[place, c], ra_sem.at[place, c], near)
        return hop(send_b.at[place, part_of], recv_b.at[place, part_of], sb_sem.at[place, c], rb_sem.at[place, c], near)

    def rs_send(side, place, with_places=()):
        send, recv = (send_a, recv_a) if side == 0 else (send_b, recv_b)
        for c in range(CHUNKS):
            lo, hi = c * size, (c + 1) * size
            value = part[OFFSETS.index(legs[side, place][0]), lo:hi, :]
            for other in with_places:
                rs_copy(side, other, c).wait_recv()
                value = value + recv[other, lo:hi, :].astype(F32)
            send[place, lo:hi, :] = value.astype(BF16)
            copy = rs_copy(side, place, c)
            copy.start()
            started.append(copy)

    def send_all(source, landing, ssem, rsem):
        def act(p):
            pltpu.make_async_remote_copy(
                src_ref=source(p), dst_ref=landing.at[g], send_sem=ssem, recv_sem=rsem,
                device_id={"group": p}, device_id_type=MESH,
            ).start()

        each_peer(act)

    def wait_rows(buffer, count, sem):
        view = buffer.at[pl.ds(0, count)]
        pltpu.make_async_copy(view, view, sem).wait()

    def wait_all(buffer, sem):
        wait_rows(buffer, NG - 1, sem)

    def text_head(h):
        for block in range(PACK // BLK):
            low, n = key_range(block)
            tok = slice(block * BLK, (block + 1) * BLK)
            lanes = slice(h * HD, (h + 1) * HD)
            scores = dot_nt(kv_v[low : low + n, 0:HD], q_v[tok, lanes]) * SCALE
            scores = jnp.where(tmask[block, 0:n, :] > 0.5, scores, -jnp.inf)
            top = jnp.max(scores, axis=0, keepdims=True)
            expo = jnp.exp(scores - top)
            dprobs = dot_nt(kv_v[low : low + n, HD : 2 * HD], og_v[tok, lanes])
            exp_t[h, block, 0:n, :] = expo
            dp_t[h, block, 0:n, :] = dprobs
            stats[h, 0:1, tok] = top
            stats[h, 1:2, tok] = jnp.sum(expo, axis=0, keepdims=True)
            stats[h, 2:3, tok] = jnp.sum(expo * dprobs, axis=0, keepdims=True)

    first_matmul(0)
    for copy in w_in[FIRST:] + small_in + other_in:
        copy.start()
    pl.semaphore_wait(barrier, 9)
    tell(0)
    rs_send(0, 0)
    first_matmul(1)
    rs_send(1, 0)
    first_matmul(2)
    rs_send(0, 1)
    for i in range(3, len(OFFSETS)):
        first_matmul(i)
    rs_send(0, 2)
    rs_send(1, 1)
    hear(0)
    tell(1)
    for copy in small_in:
        copy.wait()
    dest_row = dest_v[...].astype(F32)
    dest_col = column_of(dest_row)
    sample_col = column_of(sample_v[...].astype(F32))
    pack_row = iota((ROWS, NG), 1).astype(F32)
    tag_x[gx] = jnp.max(
        jnp.where(dest_col == pack_row, sample_col, -1.0), axis=0, keepdims=True
    )
    parity_row = (iota((1, ROWS), 1) % 2).astype(F32)
    place_out = (iota((SLOTS, ROWS), 0).astype(F32) == dest_row * 2.0 + parity_row).astype(BF16)
    parity_col = (iota((ROWS, 1), 0) % 2).astype(F32)
    place_back = (iota((ROWS, SLOTS), 1).astype(F32) == dest_col * 2.0 + parity_col).astype(BF16)

    seg_row = seg_v[...].astype(F32)
    for block in range(PACK // BLK):
        low, n = key_range(block)
        seg_key = column_of(seg_row[:, low : low + n])
        seg_tok = seg_row[:, block * BLK : (block + 1) * BLK]
        before = iota((n, BLK), 0) + low <= iota((n, BLK), 1) + block * BLK
        tmask[block, 0:n, :] = jnp.where((seg_key == seg_tok) & before, 1.0, 0.0)

    hear(1)
    tell(2)
    for dx in AROUND[:-1]:
        pltpu.make_async_remote_copy(
            src_ref=tag_x.at[gx], dst_ref=tag_x.at[gx],
            send_sem=a2a_sem.at[6], recv_sem=a2a_sem.at[7],
            device_id={"group": at(dx, 0, 0)}, device_id_type=MESH,
        ).start()
    rs_send(0, 3, (0, 1))
    rs_send(1, 2, (0,))
    hear(2)
    tell(3)
    for copy in other_in:
        copy.wait()
    text_head(0)
    hear(3)
    tell(4)
    text_head(1)
    text_head(2)
    hear(4)
    tell(5)
    text_head(3)
    hear(5)
    wait_rows(tag_x, NZ - 1, a2a_sem.at[6])
    wait_rows(tag_x, NZ - 1, a2a_sem.at[7])
    ring = pl.ds((gy * 2 + gc) * 8, 8)
    for rest in plane[:-1]:
        pltpu.make_async_remote_copy(
            src_ref=tag_x, dst_ref=tag_r.at[ring],
            send_sem=a2a_sem.at[0], recv_sem=a2a_sem.at[1],
            device_id={"group": gx * 16 + rest}, device_id_type=MESH,
        ).start()
    tag_r[ring] = tag_x[...]

    own = part[OFFSETS.index(0)]
    for side, place, recv in ((0, 2, recv_a), (1, 1, recv_b), (1, 2, recv_b), (0, 3, recv_a)):
        for c in range(CHUNKS):
            rs_copy(side, place, c).wait_recv()
        own = own + recv[place].astype(F32)
    fwd_s[...] = dot_nn(place_out, own.astype(BF16)).reshape(NG, 2, 2 * HD).astype(BF16)
    to_self = pltpu.make_async_copy(fwd_s.at[g], fwd_r.at[g], self_sem.at[0])
    to_self.start()
    send_all(lambda p: fwd_s.at[p], fwd_r, a2a_sem.at[2], a2a_sem.at[3])

    wait_rows(tag_r, NG - 8, a2a_sem.at[1])
    table = tag_r[...].reshape(NG, NG).astype(BF16)
    source = iota((SLOTS, NG), 0) // 2
    spread = ((source % 16) * 8 + source // 16 == iota((SLOTS, NG), 1)).astype(BF16)
    by_slot = dot_nn(spread, table).astype(BF16)
    mine = (iota((NG, PACK), 0) == g).astype(BF16)
    vmask[...] = jnp.where(dot_nn(by_slot, mine) == seg_row, 1.0, 0.0)

    to_self.wait()
    wait_all(fwd_r, a2a_sem.at[3])

    kv_vis[...] = fwd_r[...].astype(F32).reshape(SLOTS, 2 * HD).astype(BF16)
    for h in range(QPK):
        lanes = slice(h * HD, (h + 1) * HD)
        q_h, og_h = q_v[:, lanes], og_v[:, lanes]
        scores = dot_nt(kv_vis[:, 0:HD], q_h) * SCALE
        scores = jnp.where(vmask[...] > 0.5, scores, -jnp.inf)
        top_t = stats[h, 0:1, :]
        top = jnp.maximum(jnp.max(scores, axis=0, keepdims=True), top_t)
        expo = jnp.exp(scores - top)
        again = jnp.exp(top_t - top)
        dprobs = dot_nt(kv_vis[:, HD : 2 * HD], og_h)
        total = stats[h, 1:2, :] * again + jnp.sum(expo, axis=0, keepdims=True)
        over = 1.0 / total
        inner = (stats[h, 2:3, :] * again + jnp.sum(expo * dprobs, axis=0, keepdims=True)) * over
        probs = expo * over
        weights = probs.astype(BF16)
        dscores = (probs * (dprobs - inner) * SCALE).astype(BF16)
        p_vis[h] = weights
        ds_vis[h] = dscores
        stats[h, 3:4, :] = again * over
        stats[h, 4:5, :] = inner
        dk = dot_nn(dscores, q_h)
        dv = dot_nn(weights, og_h)
        if h == 0:
            dkv_vis[:, 0:HD] = dk
            dkv_vis[:, HD : 2 * HD] = dv
        else:
            dkv_vis[:, 0:HD] += dk
            dkv_vis[:, HD : 2 * HD] += dv

    bwd_s[...] = dkv_vis[...].reshape(NG, 2, 2 * HD).astype(BF16)
    to_self = pltpu.make_async_copy(bwd_s.at[g], bwd_r.at[g], self_sem.at[1])
    to_self.start()
    send_all(lambda p: bwd_s.at[p], bwd_r, a2a_sem.at[4], a2a_sem.at[5])

    dk_t[...] = jnp.zeros_like(dk_t)
    dv_t[...] = jnp.zeros_like(dv_t)
    for h in range(QPK):
        for block in range(PACK // BLK):
            low, n = key_range(block)
            tok = slice(block * BLK, (block + 1) * BLK)
            lanes = slice(h * HD, (h + 1) * HD)
            probs = exp_t[h, block, 0:n, :] * stats[h, 3:4, tok]
            weights = probs.astype(BF16)
            dscores = (probs * (dp_t[h, block, 0:n, :] - stats[h, 4:5, tok]) * SCALE).astype(BF16)
            dk_t[low : low + n, :] += dot_nn(dscores, q_v[tok, lanes])
            dv_t[low : low + n, :] += dot_nn(weights, og_v[tok, lanes])
            out = dot_tn(weights, kv_v[low : low + n, HD : 2 * HD])
            out = out + dot_tn(p_vis[h, :, tok], kv_vis[:, HD : 2 * HD])
            att_ref[tok, lanes] = out.astype(BF16)
            dq = dot_tn(dscores, kv_v[low : low + n, 0:HD])
            dq = dq + dot_tn(ds_vis[h, :, tok], kv_vis[:, 0:HD])
            qg_ref[tok, lanes] = dq.astype(BF16)
    tg_ref[:, 0:HD] = dk_t[...].astype(BF16)
    tg_ref[:, HD : 2 * HD] = dv_t[...].astype(BF16)

    to_self.wait()
    wait_all(bwd_r, a2a_sem.at[5])
    returned = bwd_r[...].astype(F32).reshape(SLOTS, 2 * HD).astype(BF16)
    own_kvg[...] = dot_nn(place_back, returned).astype(BF16)

    def ag_copy(side, place, c):
        part_of = pl.ds(c * size, size)
        if side == 0:
            source = own_kvg.at[part_of] if place < 2 else ag_a.at[1, part_of]
            near = left2 if place % 2 == 1 else left
            return hop(source, ag_a.at[place, part_of], ga_s.at[place, c], ga_r.at[place, c], near)
        source = own_kvg.at[part_of] if place < 2 else ag_b.at[1, part_of]
        near = right2 if place == 1 else right
        return hop(source, ag_b.at[place, part_of], gb_s.at[place, c], gb_r.at[place, c], near)

    def ag_start(*which):
        for c in range(CHUNKS):
            for side, place in which:
                if place == 3 or (side, place) == (1, 2):
                    ag_copy(side, 1, c).wait_recv()
                copy = ag_copy(side, place, c)
                copy.start()
                started.append(copy)

    def ag_block(side, place):
        block = ag_a[place] if side == 0 else ag_b[place]
        distance = place + 1 if side == 0 else -1 - place
        return dot_nt(block, w_v[OFFSETS.index(distance if distance != 4 else -4)])

    def ag_wait(side, place):
        for c in range(CHUNKS):
            ag_copy(side, place, c).wait_recv()

    ag_start((0, 1), (1, 1))
    ag_start((0, 0), (1, 0))
    acc[...] = dot_nt(own_kvg[...], w_v[OFFSETS.index(0)])
    ag_start((0, 3), (0, 2))
    ag_start((1, 2))
    acc[...] += ag_block(0, 1) + ag_block(1, 1)
    ag_wait(0, 0)
    ag_wait(1, 0)
    acc[...] += ag_block(0, 0) + ag_block(1, 0)
    ag_wait(0, 2)
    ag_wait(1, 2)
    acc[...] += ag_block(0, 2) + ag_block(1, 2)
    ag_wait(0, 3)
    vg_ref[...] = (acc[...] + ag_block(0, 3)).astype(BF16)
    for copy in started:
        copy.wait_send()
    wait_rows(tag_r, NG - 8, a2a_sem.at[0])
    wait_all(fwd_s, a2a_sem.at[2])
    wait_all(bwd_s, a2a_sem.at[4])


def write_out(*refs):
    sems = refs[8]
    copies = [pltpu.make_async_copy(refs[i], refs[4 + i], sems.at[i]) for i in range(4)]
    for copy in copies:
        copy.start()
    for copy in copies:
        copy.wait()


def on_device(
    queries, text_kv, out_grad, text_segment, visual_rows, kv_weight, visual_dest, visual_sample
):
    hbm = pl.BlockSpec(memory_space=pltpu.HBM)
    vmem = pl.BlockSpec(memory_space=pltpu.VMEM)
    sem = pltpu.SemaphoreType.DMA
    block = (ROWS, 2 * HD)
    n_blocks = PACK // BLK
    results = pl.pallas_call(
        kernel,
        out_shape=(
            jax.ShapeDtypeStruct((PACK, QPK * HD), BF16),
            jax.ShapeDtypeStruct((PACK, QPK * HD), BF16),
            jax.ShapeDtypeStruct((PACK, 2 * HD), BF16),
            jax.ShapeDtypeStruct((ROWS, kv_weight.shape[0]), BF16),
        ),
        in_specs=[hbm] * 8,
        out_specs=(vmem, vmem, vmem, vmem),
        scratch_shapes=[
            pltpu.VMEM((NZ, kv_weight.shape[0], 2 * HD), BF16),
            pltpu.VMEM(visual_rows.shape, BF16),
            pltpu.VMEM(queries.shape, BF16),
            pltpu.VMEM(text_kv.shape, BF16),
            pltpu.VMEM(out_grad.shape, BF16),
            pltpu.VMEM(text_segment.shape, jnp.int32),
            pltpu.VMEM((1, ROWS), jnp.int32),
            pltpu.VMEM((1, ROWS), jnp.int32),
            pltpu.VMEM((NZ,) + block, F32),
            pltpu.VMEM((4,) + block, BF16),
            pltpu.VMEM((4,) + block, BF16),
            pltpu.VMEM((3,) + block, BF16),
            pltpu.VMEM((3,) + block, BF16),
            pltpu.VMEM((8, 1, NG), F32),
            pltpu.VMEM((NG, 1, NG), F32),
            pltpu.VMEM((NG, 2, 2 * HD), BF16),
            pltpu.VMEM((NG, 2, 2 * HD), BF16),
            pltpu.VMEM((NG, 2, 2 * HD), BF16),
            pltpu.VMEM((NG, 2, 2 * HD), BF16),
            pltpu.VMEM(block, BF16),
            pltpu.VMEM((4,) + block, BF16),
            pltpu.VMEM((3,) + block, BF16),
            pltpu.VMEM((ROWS, kv_weight.shape[0]), F32),
            pltpu.VMEM((n_blocks, 2 * BLK, BLK), F32),
            pltpu.VMEM((SLOTS, PACK), F32),
            pltpu.VMEM((QPK, n_blocks, 2 * BLK, BLK), F32),
            pltpu.VMEM((QPK, n_blocks, 2 * BLK, BLK), F32),
            pltpu.VMEM((QPK, 8, PACK), F32),
            pltpu.VMEM((QPK, SLOTS, PACK), BF16),
            pltpu.VMEM((QPK, SLOTS, PACK), BF16),
            pltpu.VMEM((SLOTS, 2 * HD), BF16),
            pltpu.VMEM((SLOTS, 2 * HD), F32),
            pltpu.VMEM((PACK, HD), F32),
            pltpu.VMEM((PACK, HD), F32),
            sem((NZ,)),
            sem((7,)),
            sem((4, CHUNKS)),
            sem((4, CHUNKS)),
            sem((3, CHUNKS)),
            sem((3, CHUNKS)),
            sem((8,)),
            sem((2,)),
            pltpu.SemaphoreType.REGULAR((6,)),
            sem((4, CHUNKS)),
            sem((4, CHUNKS)),
            sem((3, CHUNKS)),
            sem((3, CHUNKS)),
        ],
        compiler_params=pltpu.CompilerParams(
            collective_id=0, has_side_effects=True, vmem_limit_bytes=48 << 20
        ),
        cost_estimate=pl.CostEstimate(flops=3 << 30, bytes_accessed=8 << 20, transcendentals=1 << 20),
    )(
        *(
            pltpu.with_memory_space_constraint(x, pltpu.HBM)
            for x in (
                queries, text_kv, out_grad, text_segment, visual_rows, kv_weight,
                visual_dest.reshape(1, ROWS), visual_sample.reshape(1, ROWS),
            )
        )
    )
    return pl.pallas_call(
        write_out,
        out_shape=tuple(jax.ShapeDtypeStruct(r.shape, r.dtype) for r in results),
        in_specs=[vmem] * 4,
        out_specs=(hbm,) * 4,
        scratch_shapes=[sem((4,))],
        cost_estimate=pl.CostEstimate(flops=0, bytes_accessed=2 << 20, transcendentals=0),
    )(*(pltpu.with_memory_space_constraint(r, pltpu.VMEM) for r in results))


def solution(mesh):
    placed = (
        P("group", "tensor"),
        P("group", "tensor"),
        P("group", "tensor"),
        P("group", None),
        P("group", "tensor"),
        P("tensor", None),
        P("group", None),
        P("group"),
    )
    return jax.shard_map(
        on_device,
        mesh=mesh,
        in_specs=placed,
        out_specs=(P("group", "tensor"),) * 4,
        check_vma=False,
    )
```
